512 devices in a mesh: ctx: 64 (over x, z), head: 8 (over y, core).
Axes of the slice: x: 4, y: 4, z: 16, core: 2. Of those that a mesh axis runs over, the one named last changes fastest.
Arguments:
- queries: bfloat16 [131072, 1024], P('ctx', 'head'), may hold values from -240 to 240
- key_rows: bfloat16 [131072, 128], P(('ctx', 'head')), may hold values from -7 to 7
- value_rows: bfloat16 [131072, 128], P(('ctx', 'head')), may hold values from -6 to 6
- doc_ids: int32 [131072], replicated, may hold values from 0 to 63, never falling along the last dimension, each value on 1 to 8192 neighbouring positions
Outputs:
- attended: bfloat16 [131072, 1024], P('ctx', 'head')
The draws below stay inside these ranges and needn't reach their ends.
Inputs may be any that keep to these rules, and one draw needn't show every extreme that they name: `doc_ids`: every document has between 1 and 8192 positions and one has exactly 8192; all 64 numbers occur.
All inputs are finite; a program needn't handle non-finite values.
Results may differ from the reference program's by a relative error of at most 0.0039.
Values may be sent and summed in bfloat16 or wider, within the bound.
No kernel may reach another device: no remote copies, remote signals or barrier semaphores. Data moves between devices by JAX's collectives and lax.ppermute only.
A program may use at most 64 MiB of HBM per device.

```python
import math
import jax
import jax.numpy as jnp
import numpy as np
from jax import lax

HD = 128
HQ = 8
TILE = 512
TOKENS = 131072
MAXDOC = 8192
DOCS = 64


def joint_draw(key):
    base = jax.random.fold_in(key, 11)
    first, second = jax.random.split(base, 2)
    keys_f = jnp.clip(jax.random.normal(first, (TOKENS, HD), jnp.float32), -6.0, 6.0)
    queries_f = jnp.clip(jax.random.normal(second, (TOKENS, HQ * HD), jnp.float32), -6.0, 6.0)
    return (queries_f, keys_f)


def draw_queries(key, part):
    return joint_draw(key)[0].astype(jnp.bfloat16)


def draw_key_rows(key, part):
    return joint_draw(key)[1].astype(jnp.bfloat16)


def steps_of(key, shape, cuts, smallest, top_value):
    gain = 1.0
    for position, parts in cuts:
        draws = jax.random.uniform(jax.random.fold_in(jax.random.fold_in(key, 6), position), (parts,), jnp.float32, smallest / len(cuts), top_value / len(cuts))
        gain = gain * jnp.repeat(jnp.exp(draws), shape[position] // parts).reshape((-1,) + (1,) * (len(shape) - 1 - position))
    return gain


def length_profile(count, total, reach, lean):
    portions = [(1 << 20) // math.isqrt(grade ** lean) + 1 for grade in range(2, count + 1)]
    rest, given = total - reach - (count - 1), [1] * (count - 1)
    while rest > 0:
        movable = [i for i in range(count - 1) if given[i] < reach]
        mass, left = sum([portions[i] for i in movable]), rest
        for i in movable:
            extra = min(reach - given[i], max(1, left * portions[i] // mass), rest)
            given[i] = given[i] + extra
            rest = rest - extra
    return np.array([reach] + given)


def uneven(stream_key, count, total, bound, lean):
    if count == 2:
        one = jax.random.randint(stream_key, (), max(1, total - bound), min(bound, total - 1) + 1)
        return jnp.stack([one, total - one])
    tallies = jnp.asarray(length_profile(count, total, bound, lean), jnp.int32)
    pairs = (count - 1) // 2
    donor, sink = tallies[1:1 + 2 * pairs:2], tallies[2:2 + 2 * pairs:2]
    margin = jnp.minimum(donor - 1, bound - sink)
    moved = jax.random.randint(jax.random.fold_in(stream_key, 1), (pairs,), 0, 1 << 20) % (margin + 1)
    tallies = tallies.at[1:1 + 2 * pairs:2].set(donor - moved).at[2:2 + 2 * pairs:2].set(sink + moved)
    return tallies[jax.random.permutation(jax.random.fold_in(stream_key, 2), count)]


def bell_draw(rng, shape, spread, bound, shards=(), held_as=jnp.bfloat16):
    values = jax.random.normal(rng, shape, jnp.float32) * spread
    if len(shards) > 0:
        values = steps_of(rng, shape, shards, -0.22, 0.18) * values
    return jnp.clip(values, min=-bound, max=bound).astype(held_as)


def setup_inputs(seed: int = 0) -> dict:
    key_list = jax.random.split(jax.random.key(seed), 5)
    return {
        "queries": draw_queries(jax.random.fold_in(key_list[4], 71), 0),
        "key_rows": draw_key_rows(jax.random.fold_in(key_list[4], 71), 0),
        "value_rows": bell_draw(key_list[2], (TOKENS, HD), 1.0, 6.0, ((0, 512),)),
        "doc_ids": jnp.searchsorted(jnp.cumsum(uneven(key_list[3], DOCS, TOKENS, MAXDOC, 2)), jnp.arange(TOKENS), side="right").astype(jnp.int32),
    }


def reference(queries, key_rows, value_rows, doc_ids):
    inv_root = 1.0 / math.sqrt(HD)
    window = MAXDOC + TILE
    padded_keys = jnp.concatenate([jnp.zeros((MAXDOC, HD), key_rows.dtype), key_rows], axis=0)
    padded_values = jnp.concatenate([jnp.zeros((MAXDOC, HD), value_rows.dtype), value_rows], axis=0)
    padded_ids = jnp.concatenate([jnp.full((MAXDOC,), -1, jnp.int32), doc_ids.astype(jnp.int32)])

    def one_tile(tile_index):
        start = (tile_index * TILE).astype(jnp.int32)
        query_tile = lax.dynamic_slice_in_dim(queries, start, TILE, 0).astype(jnp.float32).reshape(TILE, HQ, HD)
        key_tile = lax.dynamic_slice_in_dim(padded_keys, start, window, 0).astype(jnp.float32)
        value_tile = lax.dynamic_slice_in_dim(padded_values, start, window, 0).astype(jnp.float32)
        key_ids = lax.dynamic_slice_in_dim(padded_ids, start, window, 0)
        key_pos = start - MAXDOC + jnp.arange(window, dtype=jnp.int32)
        query_ids = lax.dynamic_slice_in_dim(doc_ids.astype(jnp.int32), start, TILE, 0)
        query_pos = start + jnp.arange(TILE, dtype=jnp.int32)
        allowed = (query_ids[:, None] == key_ids[None, :]) & (key_pos[None, :] <= query_pos[:, None])
        scores = jnp.einsum('thd,wd->htw', query_tile, key_tile, precision=lax.Precision.HIGHEST) * inv_root
        scores = jnp.where(allowed[None], scores, -jnp.inf)
        row_max = lax.optimization_barrier(jnp.max(scores, axis=-1, keepdims=True))
        weights = jnp.where(allowed[None], jnp.exp(scores - row_max), 0.0)
        totals = lax.optimization_barrier(jnp.sum(weights, axis=-1))
        rounded = lax.optimization_barrier(weights.astype(jnp.bfloat16)).astype(jnp.float32)
        mixed = jnp.einsum('htw,wd->thd', rounded, value_tile, precision=lax.Precision.HIGHEST)
        mixed = mixed / jnp.transpose(totals)[:, :, None]
        return mixed.reshape(TILE, HQ * HD).astype(jnp.bfloat16)
    tiles = lax.map(one_tile, jnp.arange(TOKENS // TILE, dtype=jnp.int32))
    return tiles.reshape(TOKENS, HQ * HD)
```

```python
import functools
import math

import jax
import jax.numpy as jnp
from jax import lax
from jax.experimental import pallas as pl
from jax.experimental.pallas import tpu as pltpu
from jax.sharding import PartitionSpec as P

PRIOR = 4
DOCS = 64
TQ = 1024
VMEM_BYTES = 24 << 20
SUB = 512
BIG = 1e30
NEG = -1e30


def ctx_shift(block, distance):
    n = lax.axis_size("ctx")
    return lax.ppermute(block, "ctx", [(i, i + distance) for i in range(n - distance)])


def y_shift(block, distance):
    n = lax.axis_size("head")
    return lax.ppermute(block, "head", [(i, (i + 2 * distance) % n) for i in range(n)])


def core_swap(block):
    n = lax.axis_size("head")
    return lax.ppermute(block, "head", [(i, i ^ 1) for i in range(n)])


def scores(q, k):
    return lax.dot_general(q, k, (((1,), (1,)), ((), ())), preferred_element_type=jnp.float32)


def halves(s):
    return [s[:, j : j + 128] for j in range(0, s.shape[1], 128)]


def allowed(base, ds, qpos, causal):
    out = []
    for j in range(2):
        kpos = base + j * 128 + lax.broadcasted_iota(jnp.int32, ds.shape, 1)
        ok = kpos >= ds
        if causal:
            ok = ok & (kpos <= qpos)
        out.append(ok)
    return out


def lazy_update(scale, rows, q_ref, m_ref, l_ref, a_ref, pieces, mask=None, init=False):
    for r in range(0, rows.size, SUB):
        at = pl.ds(pl.multiple_of(rows.start + r, SUB), SUB)
        q = q_ref[at, :]
        parts = [halves(scores(q, k)) for k, _ in pieces]
        oks = None
        if mask is not None:
            bases, ds_ref, qbase, causal = mask
            ds = ds_ref[at, :]
            qpos = qbase + rows.start + r + lax.broadcasted_iota(jnp.int32, ds.shape, 0)
            oks = [allowed(b, ds, qpos, causal) for b in bases]
        if init:
            flat = [jnp.where(ok, s, NEG) for ss, os in zip(parts, oks) for s, ok in zip(ss, os)]
            top = jnp.max(functools.reduce(jnp.maximum, flat), axis=1, keepdims=True)
            m = jnp.broadcast_to(top, (SUB, 128))
            m_ref[at, :] = m
        else:
            m = m_ref[at, :]
        probs = []
        for n, ss in enumerate(parts):
            for j, s in enumerate(ss):
                x = (s - m) * scale
                if oks is not None:
                    x = jnp.where(oks[n][j], x, NEG)
                probs.append(jnp.exp2(x))
        total = functools.reduce(jnp.add, probs)
        p = jnp.concatenate([t.astype(jnp.bfloat16) for t in probs], axis=1)
        values = jnp.concatenate([v for _, v in pieces], axis=0) if len(pieces) > 1 else pieces[0][1]
        mixed = jnp.dot(p, values, preferred_element_type=jnp.float32)
        if init:
            l_ref[at, :] = total
            a_ref[at, :] = mixed
        else:
            l_ref[at, :] += total
            a_ref[at, :] += mixed


def safe_update(scale, rows, q_ref, m_ref, l_ref, a_ref, piece, mask):
    k, v = piece
    base, ds_ref, qbase, _ = mask
    q = q_ref[rows, :]
    ds = ds_ref[rows, :]
    qpos = qbase + rows.start + lax.broadcasted_iota(jnp.int32, ds.shape, 0)
    oks = allowed(base, ds, qpos, True)
    ss = [jnp.where(ok, s, NEG) for s, ok in zip(halves(scores(q, k)), oks)]
    old = m_ref[rows, :]
    top = jnp.max(functools.reduce(jnp.maximum, ss), axis=1, keepdims=True)
    m = jnp.maximum(old, jnp.broadcast_to(top, old.shape))
    keep = jnp.exp2((old - m) * scale)
    probs = [jnp.where(ok, jnp.exp2((s - m) * scale), 0.0) for s, ok in zip(ss, oks)]
    m_ref[rows, :] = m
    l_ref[rows, :] = l_ref[rows, :] * keep + functools.reduce(jnp.add, probs)
    p = jnp.concatenate([t.astype(jnp.bfloat16) for t in probs], axis=1)
    a_ref[rows, :] = a_ref[rows, :] * keep + jnp.dot(p, v, preferred_element_type=jnp.float32)


def tile_rows(tile, size):
    return pl.ds(pl.multiple_of(tile * size, size), size)


def overflowed(l_ref, rows):
    top = jnp.max(l_ref[rows, :])
    return jnp.logical_not(top < BIG)


def split(ref, index):
    half = ref.shape[1] // 2
    return ref[index, :half, :], ref[index, half:, :]


def own_kernel(scale, tok, meta, edges, q_ref, mine, other, ds_ref, m_ref, l_ref, a_ref):
    rows_of = mine.shape[1] // 2
    size = 2 * rows_of
    lead = PRIOR * tok
    core = meta[1]

    def pair(j):
        base = lead + j * size
        return [split(mine, j), split(other, j)], [base + core * rows_of, base + (1 - core) * rows_of]

    for tile in range(tok // size):
        rows = pl.ds(tile * size, size)
        first, last = edges[2 * tile], edges[2 * tile + 1]
        pieces, bases = pair(tile)
        lazy_update(scale, rows, q_ref, m_ref, l_ref, a_ref, pieces, (bases, ds_ref, lead, True), init=True)
        if tile > 0:
            full = last <= lead
            needed = first < lead + tile * size

            def earlier(mask, tile=tile, rows=rows):
                both = [pair(j) for j in range(tile)]
                pieces = [p for ps, _ in both for p in ps]
                bases = [b for _, bs in both for b in bs]
                extra = (bases, ds_ref, lead, False) if mask else None
                lazy_update(scale, rows, q_ref, m_ref, l_ref, a_ref, pieces, extra)

            @pl.when(full)
            def _():
                earlier(False)

            @pl.when(jnp.logical_and(needed, jnp.logical_not(full)))
            def _():
                earlier(True)

    @pl.when(overflowed(l_ref, pl.ds(0, tok)))
    def _():
        @pl.loop(0, tok // size)
        def _(tile):
            rows = tile_rows(tile, size)
            m_ref[rows, :] = jnp.full((size, 128), NEG, jnp.float32)
            l_ref[rows, :] = jnp.zeros((size, 128), jnp.float32)
            a_ref[rows, :] = jnp.zeros((size, 128), jnp.float32)

            @pl.loop(0, tile + 1)
            def _(back):
                pieces, bases = pair(tile - back)
                for piece, base in zip(pieces, bases):
                    safe_update(scale, rows, q_ref, m_ref, l_ref, a_ref, piece, (base, ds_ref, lead, True))


def far_kernel(scale, tok, slots, final, meta, edges, q_ref, *refs):
    arrays = refs[: len(slots)]
    ds_ref, m_in, l_in, a_in = refs[len(slots) : len(slots) + 4]
    outs = refs[len(slots) + 4 :]
    if final:
        out_ref, m_ref, l_ref, a_ref = outs
    else:
        m_ref, l_ref, a_ref = outs
    rows_of = arrays[0].shape[1] // 2
    lead = PRIOR * tok
    per = edges.shape[0] // 2 // (tok // TQ)

    @pl.loop(0, tok // TQ)
    def _(tile):
        rows = tile_rows(tile, TQ)
        first, last = edges[2 * per * tile], edges[2 * per * (tile + 1) - 1]

        def restore():
            m_ref[rows, :] = m_in[rows, :]
            l_ref[rows, :] = l_in[rows, :]
            a_ref[rows, :] = a_in[rows, :]

        restore()

        @pl.loop(0, PRIOR)
        def _(index):
            start = lead - (index + 1) * tok
            full = start >= last
            bases = [start + rows_of * meta[slot] for slot in slots]
            wanted = [base + rows_of > first for base in bases]
            every = functools.reduce(jnp.logical_and, wanted)

            def update(which, mask):
                pieces = [split(arrays[n], index) for n in which]
                extra = ([bases[n] for n in which], ds_ref, lead, False) if mask else None
                lazy_update(scale, rows, q_ref, m_ref, l_ref, a_ref, pieces, extra)

            @pl.when(full)
            def _():
                update(range(len(slots)), False)

            @pl.when(jnp.logical_and(jnp.logical_not(full), every))
            def _():
                update(range(len(slots)), True)

            for n in range(len(slots)):

                @pl.when(jnp.logical_and(wanted[n], jnp.logical_not(every)))
                def _(n=n):
                    update([n], True)

        @pl.when(overflowed(l_ref, rows))
        def _():
            restore()

            @pl.loop(0, PRIOR)
            def _(index):
                for n, slot in enumerate(slots):
                    base = lead - (index + 1) * tok + rows_of * meta[slot]

                    @pl.when(base + rows_of > first)
                    def _(n=n, base=base):
                        safe_update(
                            scale, rows, q_ref, m_ref, l_ref, a_ref, split(arrays[n], index), (base, ds_ref, lead, True)
                        )

        if final:
            total = jnp.sum(l_ref[rows, :], axis=1, keepdims=True)
            out_ref[rows, :] = (a_ref[rows, :] / total).astype(out_ref.dtype)


SMEM = pl.BlockSpec(memory_space=pltpu.SMEM)
VMEM = pl.BlockSpec(memory_space=pltpu.VMEM)


def state_shapes(tok, hd):
    return [jax.ShapeDtypeStruct((tok, 128), jnp.float32)] * 2 + [jax.ShapeDtypeStruct((tok, hd), jnp.float32)]


def cost(tok, hd, keys):
    return pl.CostEstimate(flops=4 * tok * keys * hd, bytes_accessed=4 << 20, transcendentals=tok * keys)


def body(queries, key_rows, value_rows, doc_ids):
    tok, hd = queries.shape
    rows_of = key_rows.shape[0]
    n_head = lax.axis_size("head")
    n_y = n_head // 2
    scale = math.log2(math.e) / math.sqrt(hd)
    ctx = lax.axis_index("ctx")
    head = lax.axis_index("head")
    y, core = head // 2, head % 2

    own = jnp.concatenate([key_rows, value_rows], axis=0)
    z1 = ctx_shift(own, 1)
    z2 = ctx_shift(own, 2)

    window = jnp.concatenate([jnp.full((PRIOR * tok,), -1, jnp.int32), doc_ids])
    window = lax.dynamic_slice_in_dim(window, ctx * tok, (PRIOR + 1) * tok, 0)
    own_ids = window[PRIOR * tok :]
    docs = jnp.arange(DOCS, dtype=jnp.int32)
    counts = jnp.sum((window[None, :] < docs[:, None]).astype(jnp.int32), axis=1)
    ds = jnp.sum(jnp.where(own_ids[:, None] == docs[None, :], counts[None, :], 0), axis=1)
    edges = jnp.stack([ds[:: 2 * rows_of], ds[2 * rows_of - 1 :: 2 * rows_of]], axis=1).reshape(-1)
    ds = jnp.broadcast_to(ds[:, None], (tok, 128))
    up, down, far = (y + n_y - 1) % n_y, (y + 1) % n_y, (y + 2) % n_y
    meta = jnp.stack(
        [head, core, 2 * y + 1 - core, 2 * up + core, 2 * down + core, 2 * up + 1 - core, 2 * down + 1 - core]
        + [2 * far + core, 2 * far + 1 - core]
    ).astype(jnp.int32)

    groups = [[i for i in range(n_head) if i % 2 == c] for c in range(2)]
    mine = lax.all_gather(own[None], "head", axis=0, tiled=True, axis_index_groups=groups)
    z1, z2, mine, ds, meta, edges = lax.optimization_barrier((z1, z2, mine, ds, meta, edges))
    near = jnp.stack([z1, z2])
    beyond = ctx_shift(near, 2)
    other = core_swap(mine)

    state = pl.pallas_call(
        functools.partial(own_kernel, scale, tok),
        out_shape=state_shapes(tok, hd),
        in_specs=[SMEM, SMEM] + [VMEM] * 4,
        out_specs=[VMEM] * 3,
        cost_estimate=cost(tok, hd, tok // 2),
        compiler_params=pltpu.CompilerParams(vmem_limit_bytes=VMEM_BYTES),
        name="own_shard",
    )(meta, edges, queries, mine, other, ds)

    def step(arrays, slots, state, final=False):
        shapes = state_shapes(tok, hd)
        scratch = []
        if final:
            scratch = [pltpu.VMEM(s.shape, s.dtype) for s in shapes]
            shapes = [jax.ShapeDtypeStruct((tok, hd), queries.dtype)]
        return pl.pallas_call(
            functools.partial(far_kernel, scale, tok, slots, final),
            out_shape=shapes,
            in_specs=[SMEM, SMEM] + [VMEM] * (len(arrays) + 5),
            out_specs=[VMEM] * len(shapes),
            scratch_shapes=scratch,
            cost_estimate=cost(tok, hd, len(arrays) * PRIOR * rows_of),
            compiler_params=pltpu.CompilerParams(vmem_limit_bytes=VMEM_BYTES),
            name="far_" + "_".join(map(str, slots)),
        )(meta, edges, queries, *arrays, ds, *state)

    near, beyond, state = lax.optimization_barrier((near, beyond, state))
    z = jnp.concatenate([near, beyond], axis=0)
    zc = core_swap(z)
    yp = y_shift(z, 1)
    ym = y_shift(z, -1)
    state = step([z, zc], (0, 2), state)
    yp, ym, state = lax.optimization_barrier((yp, ym, state))
    half = PRIOR // 2
    r1 = y_shift(yp[:half], 1)
    r2 = y_shift(ym[half:], -1)
    ypc, ymc = core_swap(yp), core_swap(ym)
    state = step([yp, ym], (3, 4), state)
    r1, r2, state = lax.optimization_barrier((r1, r2, state))
    r = jnp.concatenate([r1, r2], axis=0)
    rc = core_swap(r)
    state = step([ypc, ymc], (5, 6), state)
    return step([r, rc], (7, 8), state, final=True)[0]


def solution(mesh):
    in_specs = (P("ctx", "head"), P(("ctx", "head"), None), P(("ctx", "head"), None), P())
    return jax.shard_map(body, mesh=mesh, in_specs=in_specs, out_specs=P("ctx", "head"), check_vma=False)
```

```python
import functools
import math

import jax
import jax.numpy as jnp
from jax import lax
from jax.experimental import pallas as pl
from jax.experimental.pallas import tpu as pltpu
from jax.sharding import PartitionSpec as P


PRIOR = 4
DOCS = 64
TQ = 1024
SUB = 512
SAFE = 256
NEAR = 3
HIGH = 1e30
LOW = 1e-18
NEG = -1e30
VMEM_BYTES = 24 << 20


def ctx_shift(block, distance):
    n = lax.axis_size("ctx")
    return lax.ppermute(block, "ctx", [(i, i + distance) for i in range(n - distance)])


def y_shift(block, distance):
    n = lax.axis_size("head")
    return lax.ppermute(block, "head", [(i, (i + 2 * distance) % n) for i in range(n)])


def core_swap(block):
    n = lax.axis_size("head")
    return lax.ppermute(block, "head", [(i, i ^ 1) for i in range(n)])


def score_halves(q, k):
    s = lax.dot_general(q, k, (((1,), (1,)), ((), ())), preferred_element_type=jnp.float32)
    return [s[:, j : j + 128] for j in range(0, s.shape[1], 128)]


def allowed(base, ds, qpos):
    out = []
    for j in range(2):
        kpos = base + j * 128 + lax.broadcasted_iota(jnp.int32, ds.shape, 1)
        out.append((kpos >= ds) & (kpos <= qpos))
    return out


def add_pieces(scale, rows, q_ref, ds_ref, l_ref, a_ref, lead, pieces, bases=None):
    for r in range(0, rows.size, SUB):
        at = pl.ds(pl.multiple_of(rows.start + r, SUB), SUB)
        q = q_ref[at, :]
        if bases is not None:
            ds = ds_ref[at, :]
            qpos = lead + rows.start + r + lax.broadcasted_iota(jnp.int32, ds.shape, 0)
        probs = []
        for n, (k, _) in enumerate(pieces):
            xs = [s * scale for s in score_halves(q, k)]
            if bases is not None:
                xs = [jnp.where(ok, x, NEG) for x, ok in zip(xs, allowed(bases[n], ds, qpos))]
            probs += [jnp.exp2(x) for x in xs]
        l_ref[at, :] += functools.reduce(jnp.add, probs)
        p = jnp.concatenate([t.astype(jnp.bfloat16) for t in probs], axis=1)
        values = jnp.concatenate([v for _, v in pieces], axis=0) if len(pieces) > 1 else pieces[0][1]
        a_ref[at, :] += jnp.dot(p, values, preferred_element_type=jnp.float32)


def safe_piece(scale, rows, q_ref, ds_ref, m_ref, l_ref, a_ref, lead, piece, base):
    k, v = piece
    ds = ds_ref[rows, :]
    qpos = lead + rows.start + lax.broadcasted_iota(jnp.int32, ds.shape, 0)
    oks = allowed(base, ds, qpos)
    ss = [jnp.where(ok, s, NEG) for s, ok in zip(score_halves(q_ref[rows, :], k), oks)]
    old = m_ref[rows, :]
    top = jnp.max(functools.reduce(jnp.maximum, ss), axis=1, keepdims=True)
    m = jnp.maximum(old, jnp.broadcast_to(top, old.shape))
    keep = jnp.exp2((old - m) * scale)
    probs = [jnp.where(ok, jnp.exp2((s - m) * scale), 0.0) for s, ok in zip(ss, oks)]
    m_ref[rows, :] = m
    l_ref[rows, :] = l_ref[rows, :] * keep + functools.reduce(jnp.add, probs)
    p = jnp.concatenate([t.astype(jnp.bfloat16) for t in probs], axis=1)
    a_ref[rows, :] = a_ref[rows, :] * keep + jnp.dot(p, v, preferred_element_type=jnp.float32)


def row_slice(tile, size):
    return pl.ds(pl.multiple_of(tile * size, size), size)


def split(ref, index):
    half = ref.shape[1] // 2
    return ref[index, :half, :], ref[index, half:, :]


def attend_kernel(scale, tok, count, groups, everything, first_step, meta, edges, q_ref, *refs):
    arrays = refs[:count]
    ds_ref = refs[count]
    if first_step:
        l_ref, a_ref = refs[count + 1 :]
    elif everything is None:
        l_in, a_in, l_ref, a_ref = refs[count + 1 :]
    else:
        l_in, a_in, out_ref, l_ref, a_ref, m_ref = refs[count + 1 :]
    rows_of = arrays[0].shape[1] // 2
    lead = PRIOR * tok
    per = edges.shape[0] // 2 // (tok // TQ)
    state = (q_ref, ds_ref, l_ref, a_ref, lead)

    @pl.loop(0, tok // TQ)
    def _(tile):
        rows = row_slice(tile, TQ)
        first, last = edges[2 * per * tile], edges[2 * per * (tile + 1) - 1]
        end = lead + (tile + 1) * TQ
        if first_step:
            l_ref[rows, :] = jnp.zeros((TQ, l_ref.shape[1]), jnp.float32)
            a_ref[rows, :] = jnp.zeros((TQ, a_ref.shape[1]), jnp.float32)
        else:
            l_ref[rows, :] = l_in[rows, :]
            a_ref[rows, :] = a_in[rows, :]

        for near, pieces, slots in groups:

            @pl.loop(0, pieces)
            def _(index, near=near, slots=slots):
                distance = near + index
                start = lead - distance * tok
                full = jnp.logical_and(distance > 0, start >= last)
                bases = [start + rows_of * meta[slot] for _, _, slot in slots]
                wanted = [jnp.logical_and(base + rows_of > first, base < end) for base in bases]
                every = functools.reduce(jnp.logical_and, wanted)

                def update(which, mask):
                    taken = [split(arrays[slots[n][0]], slots[n][1] + index) for n in which]
                    add_pieces(scale, rows, *state, taken, [bases[n] for n in which] if mask else None)

                @pl.when(full)
                def _():
                    update(range(len(slots)), False)

                if len(slots) > 1:

                    @pl.when(jnp.logical_and(jnp.logical_not(full), every))
                    def _():
                        update(range(len(slots)), True)

                    alone = jnp.logical_not(jnp.logical_or(full, every))
                else:
                    alone = jnp.logical_not(full)
                for n in range(len(slots)):

                    @pl.when(jnp.logical_and(wanted[n], alone))
                    def _(n=n):
                        update([n], True)

        if everything is not None:
            total = jnp.sum(l_ref[rows, :], axis=1, keepdims=True)
            good = jnp.logical_and(jnp.max(total) < HIGH, jnp.min(total) > LOW)

            @pl.when(jnp.logical_not(good))
            def _():
                @pl.loop(0, TQ // SAFE)
                def _(part):
                    some = row_slice(tile * (TQ // SAFE) + part, SAFE)
                    m_ref[some, :] = jnp.full((SAFE, m_ref.shape[1]), NEG, jnp.float32)
                    l_ref[some, :] = jnp.zeros((SAFE, l_ref.shape[1]), jnp.float32)
                    a_ref[some, :] = jnp.zeros((SAFE, a_ref.shape[1]), jnp.float32)
                    for near, pieces, slots in everything:
                        for array, offset, slot in slots:

                            @pl.loop(0, pieces)
                            def _(index, near=near, array=array, offset=offset, slot=slot):
                                base = lead - (near + index) * tok + rows_of * meta[slot]

                                @pl.when(jnp.logical_and(base + rows_of > first, base < end))
                                def _():
                                    piece = split(arrays[array], offset + index)
                                    safe_piece(scale, some, q_ref, ds_ref, m_ref, l_ref, a_ref, lead, piece, base)

            total = jnp.sum(l_ref[rows, :], axis=1, keepdims=True)
            out_ref[rows, :] = (a_ref[rows, :] / total).astype(out_ref.dtype)


def pack_kernel(k_ref, v_ref, out_ref, sems):
    rows = k_ref.shape[0]
    copies = [
        pltpu.make_async_copy(k_ref, out_ref.at[:rows, :], sems.at[0]),
        pltpu.make_async_copy(v_ref, out_ref.at[rows:, :], sems.at[1]),
    ]
    for copy in copies:
        copy.start()
    for copy in copies:
        copy.wait()


SMEM = pl.BlockSpec(memory_space=pltpu.SMEM)
VMEM = pl.BlockSpec(memory_space=pltpu.VMEM)
ANY = pl.BlockSpec(memory_space=pl.ANY)


def body(queries, key_rows, value_rows, doc_ids):
    tok, hd = queries.shape
    rows_of = key_rows.shape[0]
    n_y = lax.axis_size("head") // 2
    scale = math.log2(math.e) / math.sqrt(hd)
    ctx = lax.axis_index("ctx")
    head = lax.axis_index("head")
    y, core = head // 2, head % 2

    own = pl.pallas_call(
        pack_kernel,
        out_shape=jax.ShapeDtypeStruct((2 * rows_of, hd), key_rows.dtype),
        in_specs=[ANY] * 2,
        out_specs=VMEM,
        scratch_shapes=[pltpu.SemaphoreType.DMA((2,))],
        compiler_params=pltpu.CompilerParams(vmem_limit_bytes=1 << 20),
        name="pack",
    )(key_rows, value_rows)
    z1 = ctx_shift(own, 1)
    z2 = ctx_shift(own, 2)

    window = jnp.concatenate([jnp.full((PRIOR * tok,), -1, jnp.int32), doc_ids])
    window = lax.optimization_barrier(lax.dynamic_slice_in_dim(window, ctx * tok, (PRIOR + 1) * tok, 0))
    own_ids = window[PRIOR * tok :]
    docs = jnp.arange(DOCS, dtype=jnp.int32)
    counts = jnp.sum((window[None, :] < docs[:, None]).astype(jnp.int32), axis=1)
    ds = jnp.sum(jnp.where(own_ids[:, None] == docs[None, :], counts[None, :], 0), axis=1)
    edges = jnp.stack([ds[:: 2 * rows_of], ds[2 * rows_of - 1 :: 2 * rows_of]], axis=1).reshape(-1)
    ds = jnp.broadcast_to(ds[:, None], (tok, 128))
    up, down, far = (y + n_y - 1) % n_y, (y + 1) % n_y, (y + 2) % n_y
    meta = jnp.stack(
        [head, core, 2 * y + 1 - core, 2 * up + core, 2 * down + core, 2 * up + 1 - core, 2 * down + 1 - core]
        + [2 * far + core, 2 * far + 1 - core]
    ).astype(jnp.int32)
    z1, z2, ds, meta, edges = lax.optimization_barrier((z1, z2, ds, meta, edges))

    near = jnp.stack([z1, z2])
    g1 = jnp.stack([own, z1, z2])
    g2 = ctx_shift(near, 2)
    up1 = y_shift(g1, 1)
    down1 = y_shift(g1, -1)

    def step(arrays, groups, state, everything=None):
        shapes = [jax.ShapeDtypeStruct((tok, 128), jnp.float32), jax.ShapeDtypeStruct((tok, hd), jnp.float32)]
        scratch = []
        if everything is not None:
            scratch = [pltpu.VMEM(s.shape, s.dtype) for s in shapes + shapes[:1]]
            shapes = [jax.ShapeDtypeStruct((tok, hd), queries.dtype)]
        keys = sum(pieces * len(slots) * rows_of for _, pieces, slots in groups)
        return pl.pallas_call(
            functools.partial(attend_kernel, scale, tok, len(arrays), groups, everything, not state),
            out_shape=shapes,
            in_specs=[SMEM, SMEM] + [VMEM] * (len(arrays) + 2 + len(state)),
            out_specs=[VMEM] * len(shapes),
            scratch_shapes=scratch,
            cost_estimate=pl.CostEstimate(
                flops=4 * tok * keys * hd, bytes_accessed=4 << 20, transcendentals=tok * keys
            ),
            compiler_params=pltpu.CompilerParams(vmem_limit_bytes=VMEM_BYTES),
        )(meta, edges, queries, *arrays, ds, *state)

    count = PRIOR + 1
    far_count = count - NEAR
    state = step([g1], [(0, NEAR, [(0, 0, 0)])], [])
    up1, g2, state = lax.optimization_barrier((up1, g2, state))
    down2 = y_shift(g2, -1)
    up2 = y_shift(g2, 1)
    far1 = y_shift(up1, 1)
    state = step([up1, down1], [(0, NEAR, [(0, 0, 3), (1, 0, 4)])], state)
    down2, state = lax.optimization_barrier((down2, state))
    far2 = y_shift(down2, -1)
    state = step([g2, up2, down2], [(NEAR, far_count, [(0, 0, 0), (1, 0, 3), (2, 0, 4)])], state)
    far1, far2, state = lax.optimization_barrier((far1, far2, state))
    held = jnp.concatenate([g1, g2, up1, up2, down1, down2, far1, far2], axis=0)
    crossed = core_swap(held)
    state = step([held], [(0, count, [(0, 3 * count, 7)])], state)
    groups = [(0, count, [(0, n * count, slot) for n, slot in enumerate((2, 5, 6, 8))])]
    earlier = [(0, count, [(1, n * count, slot) for n, slot in enumerate((0, 3, 4, 7))])]
    return step([crossed, held], groups, state, everything=groups + earlier)[0]


def solution(mesh):
    in_specs = (P("ctx", "head"), P(("ctx", "head"), None), P(("ctx", "head"), None), P())
    return jax.shard_map(body, mesh=mesh, in_specs=in_specs, out_specs=P("ctx", "head"), check_vma=False)
```

```python
import functools
import math

import jax
import jax.numpy as jnp
from jax import lax
from jax.experimental import pallas as pl
from jax.experimental.pallas import tpu as pltpu
from jax.sharding import PartitionSpec as P


PRIOR = 4
DOCS = 64
TQ = 1024
SUB = 512
SAFE = 256
NEAR = 3
HIGH = 1e30
LOW = 1e-18
NEG = -1e30
VMEM_BYTES = 24 << 20


def ctx_shift(block, distance):
    n = lax.axis_size("ctx")
    return lax.ppermute(block, "ctx", [(i, i + distance) for i in range(n - distance)])


def y_shift(block, distance):
    n = lax.axis_size("head")
    return lax.ppermute(block, "head", [(i, (i + 2 * distance) % n) for i in range(n)])


def core_swap(block):
    n = lax.axis_size("head")
    return lax.ppermute(block, "head", [(i, i ^ 1) for i in range(n)])


def score_halves(q, k):
    s = lax.dot_general(q, k, (((1,), (1,)), ((), ())), preferred_element_type=jnp.float32)
    return [s[:, j : j + 128] for j in range(0, s.shape[1], 128)]


def allowed(base, ds, qpos):
    out = []
    for j in range(2):
        kpos = base + j * 128 + lax.broadcasted_iota(jnp.int32, ds.shape, 1)
        out.append((kpos >= ds) & (kpos <= qpos))
    return out


def add_pieces(scale, rows, q_ref, ds_ref, l_ref, a_ref, lead, pieces, bases=None):
    for r in range(0, rows.size, SUB):
        at = pl.ds(pl.multiple_of(rows.start + r, SUB), SUB)
        q = q_ref[at, :]
        if bases is not None:
            ds = ds_ref[at, :]
            qpos = lead + rows.start + r + lax.broadcasted_iota(jnp.int32, ds.shape, 0)
        probs = []
        for n, (k, _) in enumerate(pieces):
            xs = [s * scale for s in score_halves(q, k)]
            if bases is not None:
                xs = [jnp.where(ok, x, NEG) for x, ok in zip(xs, allowed(bases[n], ds, qpos))]
            probs += [jnp.exp2(x) for x in xs]
        l_ref[at, :] += functools.reduce(jnp.add, probs)
        p = jnp.concatenate([t.astype(jnp.bfloat16) for t in probs], axis=1)
        values = jnp.concatenate([v for _, v in pieces], axis=0) if len(pieces) > 1 else pieces[0][1]
        a_ref[at, :] += jnp.dot(p, values, preferred_element_type=jnp.float32)


def safe_piece(scale, rows, q_ref, ds_ref, m_ref, l_ref, a_ref, lead, piece, base):
    k, v = piece
    ds = ds_ref[rows, :]
    qpos = lead + rows.start + lax.broadcasted_iota(jnp.int32, ds.shape, 0)
    oks = allowed(base, ds, qpos)
    ss = [jnp.where(ok, s, NEG) for s, ok in zip(score_halves(q_ref[rows, :], k), oks)]
    old = m_ref[rows, :]
    top = jnp.max(functools.reduce(jnp.maximum, ss), axis=1, keepdims=True)
    m = jnp.maximum(old, jnp.broadcast_to(top, old.shape))
    keep = jnp.exp2((old - m) * scale)
    probs = [jnp.where(ok, jnp.exp2((s - m) * scale), 0.0) for s, ok in zip(ss, oks)]
    m_ref[rows, :] = m
    l_ref[rows, :] = l_ref[rows, :] * keep + functools.reduce(jnp.add, probs)
    p = jnp.concatenate([t.astype(jnp.bfloat16) for t in probs], axis=1)
    a_ref[rows, :] = a_ref[rows, :] * keep + jnp.dot(p, v, preferred_element_type=jnp.float32)


def row_slice(tile, size):
    return pl.ds(pl.multiple_of(tile * size, size), size)


def split(ref, index):
    half = ref.shape[1] // 2
    return ref[index, :half, :], ref[index, half:, :]


def attend_kernel(scale, tok, count, groups, everything, first_step, meta, edges, q_ref, *refs):
    arrays = refs[:count]
    ds_ref = refs[count]
    if first_step:
        l_ref, a_ref = refs[count + 1 :]
    elif everything is None:
        l_in, a_in, l_ref, a_ref = refs[count + 1 :]
    else:
        l_in, a_in, out_ref, l_ref, a_ref, m_ref = refs[count + 1 :]
    rows_of = arrays[0].shape[1] // 2
    lead = PRIOR * tok
    per = edges.shape[0] // 2 // (tok // TQ)
    state = (q_ref, ds_ref, l_ref, a_ref, lead)

    @pl.loop(0, tok // TQ)
    def _(tile):
        rows = row_slice(tile, TQ)
        first, last = edges[2 * per * tile], edges[2 * per * (tile + 1) - 1]
        end = lead + (tile + 1) * TQ
        if first_step:
            l_ref[rows, :] = jnp.zeros((TQ, l_ref.shape[1]), jnp.float32)
            a_ref[rows, :] = jnp.zeros((TQ, a_ref.shape[1]), jnp.float32)
        else:
            l_ref[rows, :] = l_in[rows, :]
            a_ref[rows, :] = a_in[rows, :]

        for near, pieces, slots in groups:

            @pl.loop(0, pieces)
            def _(index, near=near, slots=slots):
                distance = near + index
                start = lead - distance * tok
                deepest = start - max(more for _, _, _, more in slots) * tok
                full = jnp.logical_and(distance > 0, deepest >= last)
                bases = [start - more * tok + rows_of * meta[slot] for _, _, slot, more in slots]
                wanted = [jnp.logical_and(base + rows_of > first, base < end) for base in bases]
                every = functools.reduce(jnp.logical_and, wanted)

                def update(which, mask):
                    taken = [split(arrays[slots[n][0]], slots[n][1] + index) for n in which]
                    add_pieces(scale, rows, *state, taken, [bases[n] for n in which] if mask else None)

                @pl.when(full)
                def _():
                    update(range(len(slots)), False)

                if len(slots) > 1:

                    @pl.when(jnp.logical_and(jnp.logical_not(full), every))
                    def _():
                        update(range(len(slots)), True)

                    alone = jnp.logical_not(jnp.logical_or(full, every))
                else:
                    alone = jnp.logical_not(full)
                for n in range(len(slots)):

                    @pl.when(jnp.logical_and(wanted[n], alone))
                    def _(n=n):
                        update([n], True)

        if everything is not None:
            def finish(total):
                out_ref[rows, :] = (a_ref[rows, :] / total).astype(out_ref.dtype)

            total = jnp.sum(l_ref[rows, :], axis=1, keepdims=True)
            good = jnp.logical_and(jnp.max(total) < HIGH, jnp.min(total) > LOW)
            finish(total)

            @pl.when(jnp.logical_not(good))
            def _():
                @pl.loop(0, TQ // SAFE)
                def _(part):
                    some = row_slice(tile * (TQ // SAFE) + part, SAFE)
                    m_ref[some, :] = jnp.full((SAFE, m_ref.shape[1]), NEG, jnp.float32)
                    l_ref[some, :] = jnp.zeros((SAFE, l_ref.shape[1]), jnp.float32)
                    a_ref[some, :] = jnp.zeros((SAFE, a_ref.shape[1]), jnp.float32)
                    for near, pieces, slots in everything:
                        for array, offset, slot, more in slots:

                            @pl.loop(0, pieces)
                            def _(index, near=near + more, array=array, offset=offset, slot=slot):
                                base = lead - (near + index) * tok + rows_of * meta[slot]

                                @pl.when(jnp.logical_and(base + rows_of > first, base < end))
                                def _():
                                    piece = split(arrays[array], offset + index)
                                    safe_piece(scale, some, q_ref, ds_ref, m_ref, l_ref, a_ref, lead, piece, base)

                finish(jnp.sum(l_ref[rows, :], axis=1, keepdims=True))


def pack_kernel(k_ref, v_ref, out_ref, sems):
    rows = k_ref.shape[0]
    copies = [
        pltpu.make_async_copy(k_ref, out_ref.at[:rows, :], sems.at[0]),
        pltpu.make_async_copy(v_ref, out_ref.at[rows:, :], sems.at[1]),
    ]
    for copy in copies:
        copy.start()
    for copy in copies:
        copy.wait()


SMEM = pl.BlockSpec(memory_space=pltpu.SMEM)
VMEM = pl.BlockSpec(memory_space=pltpu.VMEM)
ANY = pl.BlockSpec(memory_space=pl.ANY)


def body(queries, key_rows, value_rows, doc_ids):
    tok, hd = queries.shape
    rows_of = key_rows.shape[0]
    n_y = lax.axis_size("head") // 2
    scale = math.log2(math.e) / math.sqrt(hd)
    ctx = lax.axis_index("ctx")
    head = lax.axis_index("head")
    y, core = head // 2, head % 2

    own = pl.pallas_call(
        pack_kernel,
        out_shape=jax.ShapeDtypeStruct((2 * rows_of, hd), key_rows.dtype),
        in_specs=[ANY] * 2,
        out_specs=VMEM,
        scratch_shapes=[pltpu.SemaphoreType.DMA((2,))],
        compiler_params=pltpu.CompilerParams(vmem_limit_bytes=1 << 20),
        name="pack",
    )(key_rows, value_rows)
    z1 = ctx_shift(own, 1)
    z2 = ctx_shift(own, 2)

    window = jnp.concatenate([jnp.full((PRIOR * tok,), -1, jnp.int32), doc_ids])
    window = lax.optimization_barrier(lax.dynamic_slice_in_dim(window, ctx * tok, (PRIOR + 1) * tok, 0))
    own_ids = window[PRIOR * tok :]
    docs = jnp.arange(DOCS, dtype=jnp.int32)
    counts = jnp.sum((window[None, :] < docs[:, None]).astype(jnp.int32), axis=1)
    ds = jnp.sum(jnp.where(own_ids[:, None] == docs[None, :], counts[None, :], 0), axis=1)
    edges = jnp.stack([ds[:: 2 * rows_of], ds[2 * rows_of - 1 :: 2 * rows_of]], axis=1).reshape(-1)
    ds = jnp.broadcast_to(ds[:, None], (tok, 128))
    up, down, far = (y + n_y - 1) % n_y, (y + 1) % n_y, (y + 2) % n_y
    meta = jnp.stack(
        [head, core, 2 * y + 1 - core, 2 * up + core, 2 * down + core, 2 * up + 1 - core, 2 * down + 1 - core]
        + [2 * far + core, 2 * far + 1 - core]
    ).astype(jnp.int32)
    z1, z2, ds, meta, edges = lax.optimization_barrier((z1, z2, ds, meta, edges))

    near = jnp.stack([z1, z2])
    g1 = jnp.stack([own, z1, z2])
    g2 = ctx_shift(near, 2)
    up1 = y_shift(g1, 1)
    down1 = y_shift(g1, -1)

    def step(arrays, groups, state, everything=None):
        shapes = [jax.ShapeDtypeStruct((tok, 128), jnp.float32), jax.ShapeDtypeStruct((tok, hd), jnp.float32)]
        scratch = []
        if everything is not None:
            scratch = [pltpu.VMEM(s.shape, s.dtype) for s in shapes + shapes[:1]]
            shapes = [jax.ShapeDtypeStruct((tok, hd), queries.dtype)]
        keys = sum(pieces * len(slots) * rows_of for _, pieces, slots in groups)
        return pl.pallas_call(
            functools.partial(attend_kernel, scale, tok, len(arrays), groups, everything, not state),
            out_shape=shapes,
            in_specs=[SMEM, SMEM] + [VMEM] * (len(arrays) + 2 + len(state)),
            out_specs=[VMEM] * len(shapes),
            scratch_shapes=scratch,
            cost_estimate=pl.CostEstimate(
                flops=4 * tok * keys * hd, bytes_accessed=4 << 20, transcendentals=tok * keys
            ),
            compiler_params=pltpu.CompilerParams(vmem_limit_bytes=VMEM_BYTES),
        )(meta, edges, queries, *arrays, ds, *state)

    count = PRIOR + 1
    far_count = count - NEAR
    state = step([g1], [(0, 1, [(0, 0, 0, 0)]), (1, 1, [(0, 1, 0, 0), (0, 2, 0, 1)])], [])
    up1, g2, state = lax.optimization_barrier((up1, g2, state))
    down2 = y_shift(g2, -1)
    up2 = y_shift(g2, 1)
    far1 = y_shift(up1, 1)
    both = [(0, 1, 3, 0), (1, 1, 4, 0), (0, 2, 3, 1), (1, 2, 4, 1)]
    state = step([up1, down1], [(0, 1, [(0, 0, 3, 0), (1, 0, 4, 0)]), (1, 1, both)], state)
    down2, state = lax.optimization_barrier((down2, state))
    far2 = y_shift(down2, -1)
    state = step([g2, up2, down2], [(NEAR, far_count, [(0, 0, 0, 0), (1, 0, 3, 0), (2, 0, 4, 0)])], state)
    far1, far2, state = lax.optimization_barrier((far1, far2, state))
    held = jnp.concatenate([g1, g2, up1, up2, down1, down2, far1, far2], axis=0)
    crossed = core_swap(held)
    at = 3 * count
    pairs = [(d, 1, [(0, at + d, 7, 0), (0, at + d + 1, 7, 1)]) for d in (1, 3)]
    state = step([held], [(0, 1, [(0, at, 7, 0)])] + pairs, state)
    groups = [(0, count, [(0, n * count, slot, 0) for n, slot in enumerate((2, 5, 6, 8))])]
    earlier = [(0, count, [(1, n * count, slot, 0) for n, slot in enumerate((0, 3, 4, 7))])]
    return step([crossed, held], groups, state, everything=groups + earlier)[0]


def solution(mesh):
    in_specs = (P("ctx", "head"), P(("ctx", "head"), None), P(("ctx", "head"), None), P())
    return jax.shard_map(body, mesh=mesh, in_specs=in_specs, out_specs=P("ctx", "head"), check_vma=False)
```
